32 devices in a mesh: wide: 16 (over z, x, core), narrow: 2 (over y).
Axes of the slice: x: 2, y: 2, z: 4, core: 2. Of those that a mesh axis runs over, the one named last changes fastest.
Arguments:
- amplitudes: float32 [48, 1024, 1024], P('wide', None, 'narrow'), may hold values from -24 to 24
- integrals: float32 [16, 16, 1024, 1024], P('narrow', None, 'wide'), may hold values from -0.005859375 to 0.005859375
- pair_index: int32 [48, 2], P('wide'), may hold values from 0 to 199
- window_virtuals: int32 [16], replicated, may hold values from 0 to 1023
- occ_energy: float32 [200], replicated, may hold values from -3 to -0.5
- virt_energy: float32 [1024], replicated, may hold values from 0.3 to 6
Outputs:
- update: float32 [16, 16, 48], P('narrow', None, 'wide')
The draws below stay inside these ranges and needn't reach their ends.
All inputs are finite; a program needn't handle non-finite values.
Results may differ from the reference program's by a relative error of at most 0.00013.
Values sent between devices are 32-bit elements; how exact they have to be, the bound alone decides.
No kernel may reach another device: no remote copies, remote signals or barrier semaphores. Data moves between devices by JAX's collectives and lax.ppermute only.
A program may use at most 128 MiB of HBM per device.

```python
import math
import jax
import jax.numpy as jnp
from jax import lax

NO = 200
NV = 1024
NW = 16
PAIRS = 48


def touch_ends(entries, own_key, smallest, high):
    shape = entries.shape
    spot = [jax.random.randint(jax.random.fold_in(own_key, axis), (), 0, shape[axis]) for axis in range(len(shape))]
    entries = entries.at[tuple(spot)].set(smallest)
    longest = shape.index(max(shape))
    spot[longest] = (spot[longest] + 1) % shape[longest]
    return entries.at[tuple(spot)].set(high)


def block_scale(rng, shape, cuts, low, largest):
    def one(axis_at, blocks):
        draws = jax.random.uniform(jax.random.fold_in(jax.random.fold_in(rng, 6), axis_at), (blocks,), jnp.float32, low / len(cuts), largest / len(cuts))
        return jnp.repeat(jnp.exp(draws), shape[axis_at] // blocks).reshape((-1,) + (1,) * (len(shape) - axis_at - 1))

    loudness = one(*cuts[0])
    for cut in cuts[1:]:
        loudness = loudness * one(*cut)
    return loudness


def normal_values(key, shape, scale, reach, shards=(), kind=jnp.bfloat16):
    values = jax.random.normal(key, shape, jnp.float32) * scale
    if len(shards) > 0:
        values = block_scale(key, shape, shards, -0.22, 0.18) * values
    return jnp.clip(values, min=-reach, max=reach).astype(kind)


def setup_inputs(seed: int = 0) -> dict:
    streams_of = jax.random.split(jax.random.key(seed), 7)
    amplitudes = normal_values(streams_of[0], (PAIRS, NV, NV), 4.0, 24.0, ((0, 16), (2, 2)), jnp.float32)
    integrals = normal_values(streams_of[1], (NW, NW, NV, NV), (NV * NV) ** -0.5, 0.005859375, ((0, 2), (2, 16)), jnp.float32)
    pair_index = touch_ends(jax.random.randint(streams_of[2], (PAIRS, 2), 0, NO), jax.random.fold_in(streams_of[2], 1), 0, NO - 1).astype(jnp.int32)
    window_virtuals = touch_ends(jax.random.randint(streams_of[3], (NW,), 0, NV), jax.random.fold_in(streams_of[3], 1), 0, NV - 1).astype(jnp.int32)
    occ_energy = jnp.clip(jax.random.uniform(streams_of[4], (NO,), jnp.float32, -3.0, -0.5), -3.0, -0.5)
    virt_energy = jnp.clip(jnp.exp(jax.random.uniform(streams_of[5], (NV,), jnp.float32, math.log(0.3), math.log(6.0))), 0.3, 6.0)
    return dict(amplitudes=amplitudes, integrals=integrals, pair_index=pair_index, window_virtuals=window_virtuals, occ_energy=occ_energy, virt_energy=virt_energy)


def reference(amplitudes, integrals, pair_index, window_virtuals, occ_energy, virt_energy):
    flat_integrals = integrals.reshape(NW * NW, NV * NV)
    flat_amplitudes = amplitudes.reshape(PAIRS, NV * NV)
    ladder = lax.dot_general(flat_integrals, flat_amplitudes, (((1,), (1,)), ((), ())),
                             precision=lax.Precision.HIGHEST,
                             preferred_element_type=jnp.float32).reshape(NW, NW, PAIRS)
    summed = ladder + jnp.transpose(ladder, (1, 0, 2))
    pair_energy = occ_energy[pair_index[:, 0]] + occ_energy[pair_index[:, 1]]
    window_energy = virt_energy[window_virtuals]
    denominator = pair_energy[None, None, :] - window_energy[:, None, None] - window_energy[None, :, None]
    return summed / denominator
```

```python
import functools

import jax
import jax.numpy as jnp
from jax import lax
from jax.experimental import pallas as pl
from jax.experimental.pallas import tpu as pltpu
from jax.sharding import PartitionSpec as P

INNER = 4
LANES = 128
GROUP = 8


def lookup(table, indices):
    matches = (indices[..., None] == jnp.arange(table.shape[0], dtype=jnp.int32)).astype(
        jnp.float32
    )
    return jnp.sum(matches * table, axis=-1)


def swap(value, axis, mask):
    size = lax.axis_size(axis)
    return lax.ppermute(value, axis, [(i, i ^ mask) for i in range(size)])


def pick(value, index, axis):
    return lax.dynamic_index_in_dim(value, index, axis, keepdims=False)


def halves(value):
    high = value.astype(jnp.bfloat16)
    low = (value - high.astype(jnp.float32)).astype(jnp.bfloat16)
    return jnp.concatenate([high, low], axis=0)


def contract_kernel(masks, near_count, narrow, partials, last, place_ref, *refs):
    refs = list(refs)
    out_ref, total, rows = refs[-3:]
    depth = refs[-4 - partials].shape[2]
    tiles = depth // LANES
    left_refs = refs[: narrow * tiles]
    near_refs = refs[narrow * tiles : narrow * tiles + near_count]
    far_refs = refs[narrow * tiles + near_count : narrow * tiles + near_count + narrow]
    partial_refs = refs[narrow * tiles + near_count + narrow : -3]
    step = pl.program_id(0)
    left_rows = left_refs[0].shape[0]
    height = rows.shape[0] // (narrow * tiles)
    pairs = height // GROUP

    @pl.when(step == 0)
    def _():
        total[...] = jnp.zeros_like(total)

    for j in range(narrow):
        for q in range(tiles):
            at = (j * tiles + q) * height
            lanes = pl.ds(q * LANES, LANES)
            for ref in near_refs:
                for core in range(ref.shape[0]):
                    count = ref.shape[2] * GROUP
                    rows[at : at + count, :] = ref[core, j, :, :, lanes].reshape(count, LANES)
                    at += count
            count = far_refs[j].shape[0] * GROUP
            rows[at : at + count, :] = far_refs[j][:, :, lanes].reshape(count, LANES)
    left_flat = [ref.reshape(left_rows * GROUP, LANES) for ref in left_refs]
    added = None
    for c in range(GROUP):
        left = [ref[pl.ds(c, left_rows, stride=GROUP), :] for ref in left_flat]
        right = [
            rows[pl.ds(n * height + c, pairs, stride=GROUP), :] for n in range(narrow * tiles)
        ]
        term = lax.dot_general(
            halves(jnp.concatenate(left, axis=1)),
            halves(jnp.concatenate(right, axis=1)),
            (((1,), (1,)), ((), ())),
            preferred_element_type=jnp.float32,
        )
        added = term if added is None else added + term
    total[...] += added

    @pl.when(step == pl.num_programs(0) - 1)
    def _():
        both = total[...]
        both = both[:left_rows] + both[left_rows:]
        turned = both.T
        value = turned[:pairs] + turned[pairs:]
        for ref in partial_refs:
            value = value + ref[...]
        if not last:
            out_ref[...] = value
        else:
            each = pairs // len(masks)
            for slot, mask in enumerate(masks):
                out_ref[place_ref[0] ^ mask] = value[slot * each : (slot + 1) * each]


def contract(place, integrals, near, far, partials, masks, start, last):
    left_rows, _, depth_all = integrals.shape
    narrow = len(far)
    depth = depth_all // narrow
    tiles = depth // LANES
    pairs = near[0].shape[0] * near[0].shape[2] * len(near) + far[0].shape[0]
    steps = far[0].shape[1] // GROUP
    first = start // GROUP

    def left_index(j, q, i, place):
        return (0, first + i, (place[1] ^ j) * tiles + q)

    in_specs = []
    for j in range(narrow):
        for q in range(tiles):
            in_specs.append(
                pl.BlockSpec((left_rows, GROUP, LANES), functools.partial(left_index, j, q))
            )
    for value in near:
        in_specs.append(
            pl.BlockSpec(value.shape[:3] + (GROUP, depth), lambda i, place: (0, 0, 0, first + i, 0))
        )
    for value in far:
        in_specs.append(pl.BlockSpec((value.shape[0], GROUP, depth), lambda i, place: (0, i, 0)))
    for value in partials:
        in_specs.append(pl.BlockSpec(value.shape, lambda i, place: (0, 0)))
    if last:
        shape = (len(masks), pairs // len(masks), left_rows)
        out_spec = pl.BlockSpec(shape, lambda i, place: (0, 0, 0))
    else:
        shape = (pairs, left_rows)
        out_spec = pl.BlockSpec(shape, lambda i, place: (0, 0))
    return pl.pallas_call(
        functools.partial(contract_kernel, masks, len(near), narrow, len(partials), last),
        out_shape=jax.ShapeDtypeStruct(shape, jnp.float32),
        grid_spec=pltpu.PrefetchScalarGridSpec(
            num_scalar_prefetch=1,
            grid=(steps,),
            in_specs=in_specs,
            out_specs=out_spec,
            scratch_shapes=[
                pltpu.VMEM((2 * left_rows, 2 * pairs), jnp.float32),
                pltpu.VMEM((pairs * GROUP * depth_all // LANES, LANES), jnp.float32),
            ],
        ),
        compiler_params=pltpu.CompilerParams(
            dimension_semantics=("arbitrary",), vmem_limit_bytes=32 << 20
        ),
        cost_estimate=pl.CostEstimate(
            flops=8 * left_rows * pairs * steps * GROUP * depth_all,
            bytes_accessed=4 * (left_rows + pairs) * steps * GROUP * depth_all,
            transcendentals=0,
        ),
    )(place, *([integrals] * (narrow * tiles)), *near, *far, *partials)


def inner_exchange(value, x_axis, place):
    core = place & 1
    high = (place >> 1) & 1
    kept = pick(value, core, x_axis + 1)
    come = swap(pick(value, 1 - core, x_axis + 1), "wide", 1)
    stay = jnp.stack([pick(kept, high, x_axis), pick(come, high, x_axis)])
    leave = jnp.stack([pick(kept, 1 - high, x_axis), pick(come, 1 - high, x_axis)])
    return stay, swap(leave, "wide", 2)


def row_chunks(rows):
    groups = rows // GROUP
    if groups < 4:
        return [GROUP] * groups
    last = max(1, groups // 8)
    middle = max(1, groups // 4)
    sizes = [groups - 2 * middle - last, middle, middle, last]
    return [size * GROUP for size in sizes]


def shards(amplitudes, integrals, pair_index, window_virtuals, occ_energy, virt_energy):
    wide = lax.axis_size("wide")
    narrow = lax.axis_size("narrow")
    outer = wide // INNER
    place = lax.axis_index("wide")
    side = lax.axis_index("narrow")
    outer_place = place // INNER
    pairs_here, _, depth = amplitudes.shape
    rows_here, window, rows, depth_all = integrals.shape
    near_masks = list(range(outer // 2))
    far_masks = list(range(outer // 2, outer))
    chunk_rows = row_chunks(rows)
    blocks = amplitudes.reshape(pairs_here, outer, 2, 2, rows, depth)

    first = chunk_rows[0]
    first_far = [
        swap(pick(blocks[..., :first, :], outer_place ^ k, 1), "wide", INNER * k)
        for k in far_masks
    ]
    near_own = []
    for k in near_masks:
        piece = pick(blocks, outer_place ^ k, 1)
        near_own.append(swap(piece, "wide", INNER * k) if k else piece)
    near_all = [
        jnp.stack([piece] + [swap(piece, "narrow", j) for j in range(1, narrow)])
        for piece in near_own
    ]
    near = []
    for piece in near_all:
        near.extend(inner_exchange(piece, 2, place))

    other = jnp.stack([pick(blocks[..., first:, :], outer_place ^ k, 1) for k in far_masks])
    other = jnp.stack(inner_exchange(other, 2, place))

    far_slots = INNER * len(far_masks) * pairs_here
    masks = [INNER * k + i for k in near_masks for i in range(INNER)]
    masks += [INNER * k + i for i in range(INNER) for k in far_masks]

    flat_integrals = integrals.reshape(rows_here * window, rows, depth_all)
    places = jnp.stack([place, side]).astype(jnp.int32)
    partials = []
    start = 0
    for number, count in enumerate(chunk_rows):
        if number == 0:
            own = jnp.stack(inner_exchange(jnp.stack(first_far), 2, place))
        else:
            begin = start - first
            own = jnp.stack(
                [
                    swap(other[:, :, n, :, begin : begin + count, :], "wide", INNER * k)
                    for n, k in enumerate(far_masks)
                ],
                axis=2,
            )
        own = own.reshape(far_slots, count, depth)
        far = [own] + [swap(own, "narrow", j) for j in range(1, narrow)]
        last = number == len(chunk_rows) - 1
        value = contract(
            places, flat_integrals, near, far, partials if last else [], masks, start, last
        )
        partials.append(value)
        start += count

    sent = jnp.broadcast_to(value[:, None], (wide, narrow) + value.shape[1:])
    sent = sent.reshape((wide * narrow,) + value.shape[1:])
    got = lax.all_to_all(sent, ("wide", "narrow"), 0, 0, tiled=True)
    got = got.reshape(wide, narrow, pairs_here, rows_here, window)
    whole = jnp.sum(got, axis=0).transpose(0, 2, 3, 1).reshape(window, window, pairs_here)
    row_start = side * rows_here
    combined = whole + jnp.transpose(whole, (1, 0, 2))
    combined = lax.dynamic_slice_in_dim(combined, row_start, rows_here, 0)
    own_virtuals = lax.dynamic_slice_in_dim(window_virtuals, row_start, rows_here, 0)
    row_energy = lookup(virt_energy, own_virtuals)
    column_energy = lookup(virt_energy, window_virtuals)
    pair_energy = lookup(occ_energy, pair_index[:, 0]) + lookup(occ_energy, pair_index[:, 1])
    denominator = (
        pair_energy[None, None, :] - row_energy[:, None, None] - column_energy[None, :, None]
    )
    return combined / denominator


def solution(mesh):
    in_specs = (
        P("wide", None, "narrow"),
        P("narrow", None, "wide", None),
        P("wide", None),
        P(),
        P(),
        P(),
    )
    out_specs = P("narrow", None, "wide")
    return jax.shard_map(shards, mesh=mesh, in_specs=in_specs, out_specs=out_specs, check_vma=False)
```

```python
import functools

import jax
import jax.numpy as jnp
from jax import lax
from jax.experimental import pallas as pl
from jax.experimental.pallas import tpu as pltpu
from jax.sharding import PartitionSpec as P

INNER = 4
LANES = 128
EARLY = 4
GROUP = 8


def lookup(table, indices):
    matches = (indices[..., None] == jnp.arange(table.shape[0], dtype=jnp.int32)).astype(
        jnp.float32
    )
    return jnp.sum(matches * table, axis=-1)


def swap(value, axis, mask):
    size = lax.axis_size(axis)
    return lax.ppermute(value, axis, [(i, i ^ mask) for i in range(size)])


def halves(value):
    high = value.astype(jnp.bfloat16)
    low = (value - high.astype(jnp.float32)).astype(jnp.bfloat16)
    return jnp.concatenate([high, low], axis=0)


def contract_kernel(masks, near_count, far_count, narrow, partials, last, place_ref, *refs):
    refs = list(refs)
    out_ref, total, rows = refs[-3:]
    near_size = narrow + 2
    depth = refs[-4 - partials].shape[-1]
    tiles = depth // LANES
    near_at = narrow * tiles
    far_at = near_at + near_count * near_size
    left_refs = refs[:near_at]
    near_refs = [
        refs[near_at + n * near_size : near_at + (n + 1) * near_size] for n in range(near_count)
    ]
    far_refs = [refs[far_at + n * narrow : far_at + (n + 1) * narrow] for n in range(far_count)]
    partial_refs = refs[far_at + far_count * narrow : -3]
    step = pl.program_id(0)
    left_rows = left_refs[0].shape[0]
    height = rows.shape[0] // (narrow * tiles)
    pairs = height // GROUP

    @pl.when(step == 0)
    def _():
        total[...] = jnp.zeros_like(total)

    for j in range(narrow):
        for q in range(tiles):
            at = (j * tiles + q) * height
            lanes = pl.ds(q * LANES, LANES)
            for own_and_come in near_refs:
                come, inward = own_and_come[narrow:]
                count = come.shape[1] * GROUP
                for part in (
                    own_and_come[j][:, 0, 0, :, lanes],
                    come[j, :, 0, :, lanes],
                    inward[0, j, :, :, lanes],
                    inward[1, j, :, :, lanes],
                ):
                    rows[at : at + count, :] = part.reshape(count, LANES)
                    at += count
            for own_and_come in far_refs:
                count = own_and_come[j].shape[0] * GROUP
                rows[at : at + count, :] = own_and_come[j][:, :, lanes].reshape(count, LANES)
                at += count
    left_flat = [ref.reshape(left_rows * GROUP, LANES) for ref in left_refs]
    added = None
    for c in range(GROUP):
        left = [ref[pl.ds(c, left_rows, stride=GROUP), :] for ref in left_flat]
        right = [
            rows[pl.ds(n * height + c, pairs, stride=GROUP), :] for n in range(narrow * tiles)
        ]
        term = lax.dot_general(
            halves(jnp.concatenate(left, axis=1)),
            halves(jnp.concatenate(right, axis=1)),
            (((1,), (1,)), ((), ())),
            preferred_element_type=jnp.float32,
        )
        added = term if added is None else added + term
    total[...] += added

    @pl.when(step == pl.num_programs(0) - 1)
    def _():
        both = total[...]
        both = both[:left_rows] + both[left_rows:]
        turned = both.T
        value = turned[:pairs] + turned[pairs:]
        for ref in partial_refs:
            value = value + ref[...]
        if not last:
            out_ref[...] = value
        else:
            each = pairs // (INNER * len(masks))
            for n, mask in enumerate(masks):
                for i in range(INNER):
                    slot = n * INNER + i
                    out_ref[place_ref[3] ^ (INNER * mask + i)] = value[
                        slot * each : (slot + 1) * each
                    ]


def in_hbm(value):
    return pltpu.with_memory_space_constraint(value, pltpu.HBM)


def contract(place, integrals, near, far, partials, masks, start, count, last):
    left_rows, _, depth_all = integrals.shape
    narrow = len(far[0][1])
    depth = depth_all // narrow
    tiles = depth // LANES
    pairs = sum(INNER * value[0].shape[0] for _, value in near)
    pairs += sum(value[0].shape[0] for _, value in far)
    steps = count // GROUP
    first = start // GROUP

    def left_index(j, q, i, place):
        return (0, first + i, (place[4] ^ j) * tiles + q)

    in_specs = []
    for j in range(narrow):
        for q in range(tiles):
            in_specs.append(
                pl.BlockSpec((left_rows, GROUP, LANES), functools.partial(left_index, j, q))
            )
    for begins, value in near:
        each = value[0].shape[0]
        own, come, inward = [(start - at) // GROUP for at in begins]
        for _ in range(narrow):
            in_specs.append(
                pl.BlockSpec(
                    (each, 1, 1, GROUP, depth),
                    lambda i, place, own=own: (0, place[1], place[0], own + i, 0),
                )
            )
        in_specs.append(
            pl.BlockSpec(
                (narrow, each, 1, GROUP, depth),
                lambda i, place, come=come: (0, 0, place[1], come + i, 0),
            )
        )
        in_specs.append(
            pl.BlockSpec(
                (2, narrow, each, GROUP, depth),
                lambda i, place, inward=inward: (0, 0, 0, inward + i, 0),
            )
        )
    for begin, value in far:
        group = (start - begin) // GROUP
        for v in value:
            in_specs.append(
                pl.BlockSpec(
                    (v.shape[0], GROUP, depth), lambda i, place, group=group: (0, group + i, 0)
                )
            )
    for value in partials:
        in_specs.append(pl.BlockSpec(value.shape, lambda i, place: (0, 0)))
    if last:
        shape = (INNER * len(masks), pairs // (INNER * len(masks)), left_rows)
        out_spec = pl.BlockSpec(shape, lambda i, place: (0, 0, 0))
    else:
        shape = (pairs, left_rows)
        out_spec = pl.BlockSpec(shape, lambda i, place: (0, 0))
    return pl.pallas_call(
        functools.partial(
            contract_kernel, masks, len(near), len(far), narrow, len(partials), last
        ),
        out_shape=jax.ShapeDtypeStruct(shape, jnp.float32),
        grid_spec=pltpu.PrefetchScalarGridSpec(
            num_scalar_prefetch=1,
            grid=(steps,),
            in_specs=in_specs,
            out_specs=out_spec,
            scratch_shapes=[
                pltpu.VMEM((2 * left_rows, 2 * pairs), jnp.float32),
                pltpu.VMEM((pairs * GROUP * depth_all // LANES, LANES), jnp.float32),
            ],
        ),
        compiler_params=pltpu.CompilerParams(
            dimension_semantics=("arbitrary",), vmem_limit_bytes=32 << 20
        ),
        cost_estimate=pl.CostEstimate(
            flops=8 * left_rows * pairs * steps * GROUP * depth_all,
            bytes_accessed=4 * (left_rows + pairs) * steps * GROUP * depth_all,
            transcendentals=0,
        ),
    )(
        place,
        *([integrals] * (narrow * tiles)),
        *[in_hbm(v) for _, value in near for v in value],
        *[in_hbm(v) for _, value in far for v in value],
        *partials,
    )


def gather_kernel(copies, source_count, place_ref, *refs):
    sources = refs[:source_count]
    outs, sems = refs[source_count:-1], refs[-1]
    started = []
    for n, (source, source_at, out, out_at) in enumerate(copies):
        copy = pltpu.make_async_copy(
            sources[source].at[source_at(place_ref)], outs[out].at[out_at], sems.at[n]
        )
        copy.start()
        started.append(copy)
    for copy in started:
        copy.wait()


def gather(place, sources, shapes, copies):
    return pl.pallas_call(
        functools.partial(gather_kernel, copies, len(sources)),
        out_shape=[jax.ShapeDtypeStruct(shape, jnp.float32) for shape in shapes],
        grid_spec=pltpu.PrefetchScalarGridSpec(
            num_scalar_prefetch=1,
            grid=(),
            in_specs=[pl.BlockSpec(memory_space=pl.ANY)] * len(sources),
            out_specs=[pl.BlockSpec(memory_space=pltpu.VMEM)] * len(shapes),
            scratch_shapes=[pltpu.SemaphoreType.DMA((len(copies),))],
        ),
        compiler_params=pltpu.CompilerParams(vmem_limit_bytes=16 << 20),
        cost_estimate=pl.CostEstimate(flops=0, bytes_accessed=0, transcendentals=0),
    )(place, *sources)


ALL = slice(None)


class Plan:
    def __init__(self, place):
        self.place = place
        self.before = []
        self.reset()

    def reset(self):
        self.sources, self.shapes, self.copies = [], [], []

    def wait(self, *values):
        self.before.extend(values)

    def after(self, value):
        value, _ = lax.optimization_barrier((value, self.before))
        return value

    def new(self, *shape):
        self.shapes.append(shape)
        return len(self.shapes) - 1

    def put(self, out, out_at, value, source_at):
        index = next((n for n, v in enumerate(self.sources) if v is value), len(self.sources))
        if index == len(self.sources):
            self.sources.append(value)
        self.copies.append((index, source_at, out, out_at))

    def run(self):
        sources = list(self.sources)
        if self.before:
            sources, _ = lax.optimization_barrier((sources, self.before))
        made = list(gather(self.place, sources, self.shapes, self.copies))
        self.before = [made[0]]
        self.reset()
        return made


def shards(amplitudes, integrals, pair_index, window_virtuals, occ_energy, virt_energy):
    wide = lax.axis_size("wide")
    narrow = lax.axis_size("narrow")
    outer = wide // INNER
    place = lax.axis_index("wide")
    side = lax.axis_index("narrow")
    outer_place = place // INNER
    pairs_here, _, depth = amplitudes.shape
    rows_here, window, rows, depth_all = integrals.shape
    near_masks = list(range(outer // 2))
    far_masks = list(range(outer // 2, outer))
    blocks = amplitudes.reshape(pairs_here, outer, 2, 2, rows, depth)

    each = pairs_here
    far_count = len(far_masks)
    places = jnp.stack(
        [place & 1, (place >> 1) & 1, outer_place, place, side]
    ).astype(jnp.int32)
    plan = Plan(places)

    def outward(value, k):
        return swap(value, "wide", INNER * k)

    def sideways(value):
        return [value] + [swap(value, "narrow", j) for j in range(1, narrow)]

    half = GROUP * max(1, EARLY * rows // (8 * GROUP))
    early, late = (0, half), (half, rows - half)

    def core_step(sides):
        leave = plan.new(len(sides), each, 2, sides[0].shape[-2], depth)
        for j, v in enumerate(sides):
            plan.put(leave, (j,), v, lambda p: (ALL, ALL, 1 - p[0]))

    def high_step(sides, come, at=0, count=None):
        count = count or come.shape[-2]
        span = pl.ds(at, count)
        leave = plan.new(2, len(sides), each, count, depth)
        for j, v in enumerate(sides):
            plan.put(leave, (0, j), v, lambda p: (ALL, 1 - p[1], p[0], span))
        plan.put(leave, (1,), come, lambda p: (ALL, ALL, 1 - p[1], span))

    def cut(k, span):
        out = plan.new(each, 2, 2, span[1], depth)
        plan.put(out, (), blocks, lambda p: (ALL, p[2] ^ k, ALL, ALL, pl.ds(*span)))

    lead = far_masks[0]
    others = near_masks[1:]
    rest = [(k, early) for k in far_masks[1:]]
    rest += [(k, late) for k in others + far_masks]

    cut(lead, early)
    first = outward(plan.run()[0], lead)
    cut(0, (0, rows))
    offsets = [sum(span[1] for _, span in rest[:n]) for n in range(len(rest) + 1)]
    leave = plan.new(each, 2, offsets[-1], depth)
    for n, (k, span) in enumerate(rest):
        plan.put(
            leave,
            (ALL, ALL, pl.ds(offsets[n], span[1])),
            blocks,
            lambda p, k=k, span=span: (ALL, p[2] ^ k, ALL, 1 - p[0], pl.ds(*span)),
        )
    for k in others:
        cut(k, early)
    made = plan.run()
    side_early = [outward(v, k) for v, k in zip(made[2:], others)]
    home = sideways(made[0])
    rest_come = swap(made[1], "wide", 1)
    for n, (k, span) in enumerate(rest):
        leave = plan.new(2, each, span[1], depth)
        plan.put(
            leave,
            (0,),
            blocks,
            lambda p, k=k, span=span: (ALL, p[2] ^ k, 1 - p[1], p[0], pl.ds(*span)),
        )
        there = pl.ds(offsets[n], span[1])
        plan.put(leave, (1,), rest_come, lambda p, there=there: (ALL, 1 - p[1], there))
    rest_in = [swap(v, "wide", 2) for v in plan.run()]

    def rest_piece(k, span, part=None):
        n = rest.index((k, span))
        at, count = part or span
        inside = pl.ds(at - span[0], count)
        rows_here = pl.ds(at, count)
        out = plan.new(2, 2, each, count, depth)
        plan.put(out, (0, 0), blocks, lambda p: (ALL, p[2] ^ k, p[1], p[0], rows_here))
        there = pl.ds(offsets[n] + at - span[0], count)
        plan.put(out, (0, 1), rest_come, lambda p: (ALL, p[1], there))
        plan.put(out, (1,), rest_in[n], lambda p: (ALL, ALL, inside))

    last_spans = [late]
    if late[1] >= 2 * GROUP:
        tail = GROUP * (late[1] // (2 * GROUP))
        last_spans = [(half, late[1] - tail), (rows - tail, tail)]
    late_parts = [(k, late) for k in far_masks[:-1]] + [(far_masks[-1], part) for part in last_spans]
    far = {k: [] for k in others + far_masks}

    def across(k, begin, value):
        sides = sideways(value.reshape(INNER * each, -1, depth))
        far[k].append((begin, sides))
        return sides[1]

    def side_pieces(span):
        for k in others:
            rest_piece(k, span)
        return [(k, span[0], outward(v, k)) for k, v in zip(others, plan.run())] if others else []

    def crossing(pieces):
        plan.wait([v for _, _, v in pieces])
        return [across(k, begin, plan.after(v)) for k, begin, v in pieces]

    plan.wait(first, side_early, rest_in[: far_count - 1 + len(others)])
    sides = [sideways(plan.after(v)) for v in side_early]
    core_step([first])
    for k in far_masks[1:]:
        rest_piece(k, early)
    made = plan.run()
    going = [(k, 0, outward(v, k)) for k, v in zip(far_masks[1:], made[1:])]
    come = swap(made[0], "wide", 1)
    high_step([first], come)
    inward = swap(plan.run()[0], "wide", 2)
    plan.wait(rest_in)
    own = plan.new(2, 2, each, half, depth)
    plan.put(own, (0, 0), first, lambda p: (ALL, p[1], p[0]))
    plan.put(own, (0, 1), come, lambda p: (0, ALL, p[1]))
    plan.put(own, (1,), inward, lambda p: (ALL, 0))
    lead_own = plan.run()[0]
    plan.wait(home[1])
    crossed = [v[1] for v in sides]
    lead_crossed = across(lead, 0, lead_own)
    side_late = side_pieces(late)

    for k, part in late_parts:
        rest_piece(k, late, part)
    plan.wait([v for _, _, v in going])
    late_out = plan.run()
    later = [
        (k, late[0], outward(v, k)) for (k, _), v in zip(late_parts[: far_count - 1], late_out)
    ]
    plan.wait(crossed)
    crossed = crossing(going)
    for v in [home] + sides:
        core_step(v)
    comes = [swap(v, "wide", 1) for v in plan.run()]
    high_step(home, comes[0], *early)
    for v, come in zip(sides, comes[1:]):
        high_step(v, come)
    high_step(home, comes[0], *late)
    made = plan.run()
    inner = [swap(v, "wide", 2) for v in made[:-1]]
    plan.wait(lead_crossed)
    side_crossed = crossing(side_late)

    plan.wait(crossed, inner[0])
    home_late = swap(plan.after(made[-1]), "wide", 2)
    final = [(far_masks[-1], part) for part in last_spans]
    final_out = late_out[far_count - 1 :]
    plan.wait([v for _, _, v in later])
    ending = [
        (k, part[0], outward(plan.after(v), k)) for (k, part), v in zip(final[:1], final_out)
    ]
    crossed = crossing(later)

    flat_integrals = integrals.reshape(rows_here * window, rows, depth_all)
    partials = []
    near = [[((0, 0, 0), v + [c, i]) for v, c, i in zip([home] + sides, comes, inner)]]
    near.append([((0, 0, late[0]), home + [comes[0], home_late])])

    def multiply(h, span, last):
        pieces = [
            next(v for v in reversed(far[k]) if v[0] <= span[0])
            for k in (others if h else []) + far_masks
        ]
        value = contract(
            places,
            plan.after(flat_integrals),
            near[h],
            pieces,
            partials if last else [],
            near_masks + far_masks,
            *span,
            last,
        )
        plan.before = [value]
        partials.append(value)

    multiply(0, early, False)
    plan.wait(side_crossed)
    crossing(ending)
    for (k, part), v in zip(final[1:], final_out[1:]):
        ending = [(k, part[0], outward(plan.after(v), k))]
    if final[1:]:
        crossing(ending)
    for n, part in enumerate(last_spans):
        multiply(1, part, n == len(last_spans) - 1)
    value = partials[-1]

    sent = jnp.broadcast_to(value[:, None], (wide, narrow) + value.shape[1:])
    sent = sent.reshape((wide * narrow,) + value.shape[1:])
    got = lax.all_to_all(sent, ("wide", "narrow"), 0, 0, tiled=True)
    got = got.reshape(wide, narrow, pairs_here, rows_here, window)
    whole = jnp.sum(got, axis=0).transpose(0, 2, 3, 1).reshape(window, window, pairs_here)
    row_start = side * rows_here
    combined = whole + jnp.transpose(whole, (1, 0, 2))
    combined = lax.dynamic_slice_in_dim(combined, row_start, rows_here, 0)
    own_virtuals = lax.dynamic_slice_in_dim(window_virtuals, row_start, rows_here, 0)
    row_energy = lookup(virt_energy, own_virtuals)
    column_energy = lookup(virt_energy, window_virtuals)
    pair_energy = lookup(occ_energy, pair_index[:, 0]) + lookup(occ_energy, pair_index[:, 1])
    denominator = (
        pair_energy[None, None, :] - row_energy[:, None, None] - column_energy[None, :, None]
    )
    return combined / denominator


def solution(mesh):
    in_specs = (
        P("wide", None, "narrow"),
        P("narrow", None, "wide", None),
        P("wide", None),
        P(),
        P(),
        P(),
    )
    out_specs = P("narrow", None, "wide")
    return jax.shard_map(shards, mesh=mesh, in_specs=in_specs, out_specs=out_specs, check_vma=False)
```

```python
import functools

import jax
import jax.numpy as jnp
from jax import lax
from jax.experimental import pallas as pl
from jax.experimental.pallas import tpu as pltpu
from jax.sharding import PartitionSpec as P

INNER = 4
LANES = 128
EARLY = 4
GROUP = 8


def lookup(table, indices):
    matches = (indices[..., None] == jnp.arange(table.shape[0], dtype=jnp.int32)).astype(
        jnp.float32
    )
    return jnp.sum(matches * table, axis=-1)


def swap(value, axis, mask):
    size = lax.axis_size(axis)
    return lax.ppermute(value, axis, [(i, i ^ mask) for i in range(size)])


def halves(value):
    high = value.astype(jnp.bfloat16)
    low = (value - high.astype(jnp.float32)).astype(jnp.bfloat16)
    return jnp.concatenate([high, low], axis=0)


def contract_kernel(masks, near_count, far_count, narrow, partials, last, place_ref, *refs):
    refs = list(refs)
    out_ref, total, rows = refs[-3:]
    near_size = narrow + 2
    depth = refs[-4 - partials].shape[-1]
    tiles = depth // LANES
    near_at = narrow * tiles
    far_at = near_at + near_count * near_size
    left_refs = refs[:near_at]
    near_refs = [
        refs[near_at + n * near_size : near_at + (n + 1) * near_size] for n in range(near_count)
    ]
    far_refs = [refs[far_at + n * narrow : far_at + (n + 1) * narrow] for n in range(far_count)]
    partial_refs = refs[far_at + far_count * narrow : -3]
    step = pl.program_id(0)
    left_rows = left_refs[0].shape[0]
    height = rows.shape[0] // (narrow * tiles)
    pairs = height // GROUP

    @pl.when(step == 0)
    def _():
        total[...] = jnp.zeros_like(total)

    for j in range(narrow):
        for q in range(tiles):
            at = (j * tiles + q) * height
            lanes = pl.ds(q * LANES, LANES)
            for own_and_come in near_refs:
                come, inward = own_and_come[narrow:]
                count = come.shape[1] * GROUP
                for part in (
                    own_and_come[j][:, 0, 0, :, lanes],
                    come[j, :, 0, :, lanes],
                    inward[0, j, :, :, lanes],
                    inward[1, j, :, :, lanes],
                ):
                    rows[at : at + count, :] = part.reshape(count, LANES)
                    at += count
            for own_and_come in far_refs:
                count = own_and_come[j].shape[0] * GROUP
                rows[at : at + count, :] = own_and_come[j][:, :, lanes].reshape(count, LANES)
                at += count
    left_flat = [ref.reshape(left_rows * GROUP, LANES) for ref in left_refs]
    added = None
    for c in range(GROUP):
        left = [ref[pl.ds(c, left_rows, stride=GROUP), :] for ref in left_flat]
        right = [
            rows[pl.ds(n * height + c, pairs, stride=GROUP), :] for n in range(narrow * tiles)
        ]
        term = lax.dot_general(
            halves(jnp.concatenate(left, axis=1)),
            halves(jnp.concatenate(right, axis=1)),
            (((1,), (1,)), ((), ())),
            preferred_element_type=jnp.float32,
        )
        added = term if added is None else added + term
    total[...] += added

    @pl.when(step == pl.num_programs(0) - 1)
    def _():
        both = total[...]
        both = both[:left_rows] + both[left_rows:]
        turned = both.T
        value = turned[:pairs] + turned[pairs:]
        for ref in partial_refs:
            value = value + ref[...]
        if not last:
            out_ref[...] = value
        else:
            each = pairs // (INNER * len(masks))
            for n, mask in enumerate(masks):
                for i in range(INNER):
                    slot = n * INNER + i
                    piece = value[slot * each : (slot + 1) * each]
                    for j in range(narrow):
                        out_ref[place_ref[3] ^ (INNER * mask + i), j] = piece


def in_hbm(value):
    return pltpu.with_memory_space_constraint(value, pltpu.HBM)


def contract(place, integrals, near, far, partials, masks, start, count, last):
    left_rows, _, depth_all = integrals.shape
    narrow = len(far[0][1])
    depth = depth_all // narrow
    tiles = depth // LANES
    pairs = sum(INNER * value[0].shape[0] for _, value in near)
    pairs += sum(value[0].shape[0] for _, value in far)
    steps = count // GROUP
    first = start // GROUP

    def left_index(j, q, i, place):
        return (0, first + i, (place[4] ^ j) * tiles + q)

    in_specs = []
    for j in range(narrow):
        for q in range(tiles):
            in_specs.append(
                pl.BlockSpec((left_rows, GROUP, LANES), functools.partial(left_index, j, q))
            )
    for begins, value in near:
        each = value[0].shape[0]
        own, come, inward = [(start - at) // GROUP for at in begins]
        for _ in range(narrow):
            in_specs.append(
                pl.BlockSpec(
                    (each, 1, 1, GROUP, depth),
                    lambda i, place, own=own: (0, place[1], place[0], own + i, 0),
                )
            )
        in_specs.append(
            pl.BlockSpec(
                (narrow, each, 1, GROUP, depth),
                lambda i, place, come=come: (0, 0, place[1], come + i, 0),
            )
        )
        in_specs.append(
            pl.BlockSpec(
                (2, narrow, each, GROUP, depth),
                lambda i, place, inward=inward: (0, 0, 0, inward + i, 0),
            )
        )
    for begin, value in far:
        group = (start - begin) // GROUP
        for v in value:
            in_specs.append(
                pl.BlockSpec(
                    (v.shape[0], GROUP, depth), lambda i, place, group=group: (0, group + i, 0)
                )
            )
    for value in partials:
        in_specs.append(pl.BlockSpec(value.shape, lambda i, place: (0, 0)))
    if last:
        shape = (INNER * len(masks), narrow, pairs // (INNER * len(masks)), left_rows)
        out_spec = pl.BlockSpec(shape, lambda i, place: (0, 0, 0, 0))
    else:
        shape = (pairs, left_rows)
        out_spec = pl.BlockSpec(shape, lambda i, place: (0, 0))
    return pl.pallas_call(
        functools.partial(
            contract_kernel, masks, len(near), len(far), narrow, len(partials), last
        ),
        out_shape=jax.ShapeDtypeStruct(shape, jnp.float32),
        grid_spec=pltpu.PrefetchScalarGridSpec(
            num_scalar_prefetch=1,
            grid=(steps,),
            in_specs=in_specs,
            out_specs=out_spec,
            scratch_shapes=[
                pltpu.VMEM((2 * left_rows, 2 * pairs), jnp.float32),
                pltpu.VMEM((pairs * GROUP * depth_all // LANES, LANES), jnp.float32),
            ],
        ),
        compiler_params=pltpu.CompilerParams(
            dimension_semantics=("arbitrary",), vmem_limit_bytes=32 << 20
        ),
        cost_estimate=pl.CostEstimate(
            flops=8 * left_rows * pairs * steps * GROUP * depth_all,
            bytes_accessed=4 * (left_rows + pairs) * steps * GROUP * depth_all,
            transcendentals=0,
        ),
    )(
        place,
        *([integrals] * (narrow * tiles)),
        *[in_hbm(v) for _, value in near for v in value],
        *[v for _, value in far for v in value],
        *partials,
    )


def gather_kernel(copies, source_count, place_ref, *refs):
    sources = refs[:source_count]
    outs, sems = refs[source_count:-1], refs[-1]
    started = []
    for n, (source, source_at, out, out_at) in enumerate(copies):
        copy = pltpu.make_async_copy(
            sources[source].at[source_at(place_ref)], outs[out].at[out_at], sems.at[n]
        )
        copy.start()
        started.append(copy)
    for copy in started:
        copy.wait()


def gather(place, sources, shapes, copies, pinned):
    return pl.pallas_call(
        functools.partial(gather_kernel, copies, len(sources)),
        out_shape=[jax.ShapeDtypeStruct(shape, jnp.float32) for shape in shapes],
        grid_spec=pltpu.PrefetchScalarGridSpec(
            num_scalar_prefetch=1,
            grid=(),
            in_specs=[
                pl.BlockSpec(memory_space=pltpu.HBM if n in pinned else pl.ANY)
                for n in range(len(sources))
            ],
            out_specs=[pl.BlockSpec(memory_space=pltpu.VMEM)] * len(shapes),
            scratch_shapes=[pltpu.SemaphoreType.DMA((len(copies),))],
        ),
        compiler_params=pltpu.CompilerParams(vmem_limit_bytes=16 << 20),
        cost_estimate=pl.CostEstimate(flops=0, bytes_accessed=0, transcendentals=0),
    )(place, *sources)


ALL = slice(None)


class Plan:
    def __init__(self, place, large):
        self.place = place
        self.large = large
        self.before = []
        self.reset()

    def reset(self):
        self.sources, self.shapes, self.copies = [], [], []

    def wait(self, *values):
        self.before.extend(values)

    def after(self, value):
        value, _ = lax.optimization_barrier((value, self.before))
        return value

    def new(self, *shape):
        self.shapes.append(shape)
        return len(self.shapes) - 1

    def put(self, out, out_at, value, source_at):
        index = next((n for n, v in enumerate(self.sources) if v is value), len(self.sources))
        if index == len(self.sources):
            self.sources.append(value)
        self.copies.append((index, source_at, out, out_at))

    def run(self):
        sources = list(self.sources)
        pinned = [n for n, v in enumerate(sources) if v is self.large]
        if self.before:
            sources, _ = lax.optimization_barrier((sources, self.before))
        sources = [in_hbm(v) if n in pinned else v for n, v in enumerate(sources)]
        made = list(gather(self.place, sources, self.shapes, self.copies, pinned))
        self.before = [made[0]]
        self.reset()
        return made


def shards(amplitudes, integrals, pair_index, window_virtuals, occ_energy, virt_energy):
    wide = lax.axis_size("wide")
    narrow = lax.axis_size("narrow")
    outer = wide // INNER
    place = lax.axis_index("wide")
    side = lax.axis_index("narrow")
    outer_place = place // INNER
    pairs_here, _, depth = amplitudes.shape
    rows_here, window, rows, depth_all = integrals.shape
    near_masks = list(range(outer // 2))
    far_masks = list(range(outer // 2, outer))
    row_start = side * rows_here
    own_virtuals = lax.dynamic_slice_in_dim(window_virtuals, row_start, rows_here, 0)
    row_energy = lookup(virt_energy, own_virtuals)
    column_energy = lookup(virt_energy, window_virtuals)
    pair_energy = lookup(occ_energy, pair_index[:, 0]) + lookup(occ_energy, pair_index[:, 1])
    denominator = (
        pair_energy[None, None, :] - row_energy[:, None, None] - column_energy[None, :, None]
    )
    blocks = amplitudes.reshape(pairs_here, outer, 2, 2, rows, depth)

    each = pairs_here
    far_count = len(far_masks)
    places = jnp.stack(
        [place & 1, (place >> 1) & 1, outer_place, place, side]
    ).astype(jnp.int32)
    plan = Plan(places, blocks)

    def outward(value, k):
        return swap(value, "wide", INNER * k)

    def sideways(value):
        return [value] + [swap(value, "narrow", j) for j in range(1, narrow)]

    half = GROUP * max(1, EARLY * rows // (8 * GROUP))
    early, late = (0, half), (half, rows - half)

    def core_step(sides):
        leave = plan.new(len(sides), each, 2, sides[0].shape[-2], depth)
        for j, v in enumerate(sides):
            plan.put(leave, (j,), v, lambda p: (ALL, ALL, 1 - p[0]))

    def high_step(sides, come, at=0, count=None):
        count = count or come.shape[-2]
        span = pl.ds(at, count)
        leave = plan.new(2, len(sides), each, count, depth)
        for j, v in enumerate(sides):
            plan.put(leave, (0, j), v, lambda p: (ALL, 1 - p[1], p[0], span))
        plan.put(leave, (1,), come, lambda p: (ALL, ALL, 1 - p[1], span))

    def cut(k, span):
        out = plan.new(each, 2, 2, span[1], depth)
        plan.put(out, (), blocks, lambda p: (ALL, p[2] ^ k, ALL, ALL, pl.ds(*span)))

    lead = far_masks[0]
    others = near_masks[1:]
    rest = [(k, early) for k in far_masks[1:]]
    rest += [(k, late) for k in others + far_masks]

    cut(lead, early)
    first = outward(plan.run()[0], lead)
    cut(0, (0, rows))
    offsets = [sum(span[1] for _, span in rest[:n]) for n in range(len(rest) + 1)]
    leave = plan.new(each, 2, offsets[-1], depth)
    for n, (k, span) in enumerate(rest):
        plan.put(
            leave,
            (ALL, ALL, pl.ds(offsets[n], span[1])),
            blocks,
            lambda p, k=k, span=span: (ALL, p[2] ^ k, ALL, 1 - p[0], pl.ds(*span)),
        )
    for k in others:
        cut(k, early)
    made = plan.run()
    side_early = [outward(v, k) for v, k in zip(made[2:], others)]
    home = sideways(made[0])
    rest_come = swap(made[1], "wide", 1)
    single = len(rest) - far_count
    for n, (k, span) in enumerate(rest):
        there = pl.ds(offsets[n], span[1])
        if n < single:
            leave, at = plan.new(2, each, span[1], depth), ()
        else:
            if n == single:
                leave = plan.new(2, far_count, each, span[1], depth)
            at = (n - single,)
        plan.put(
            leave,
            (0,) + at,
            blocks,
            lambda p, k=k, span=span: (ALL, p[2] ^ k, 1 - p[1], p[0], pl.ds(*span)),
        )
        plan.put(leave, (1,) + at, rest_come, lambda p, there=there: (ALL, 1 - p[1], there))
    rest_in = [swap(v, "wide", 2) for v in plan.run()]

    def rest_piece(k, span, part=None):
        n = rest.index((k, span))
        at, count = part or span
        inside = pl.ds(at - span[0], count)
        rows_here = pl.ds(at, count)
        out = plan.new(2, 2, each, count, depth)
        plan.put(out, (0, 0), blocks, lambda p: (ALL, p[2] ^ k, p[1], p[0], rows_here))
        there = pl.ds(offsets[n] + at - span[0], count)
        plan.put(out, (0, 1), rest_come, lambda p: (ALL, p[1], there))
        if n < single:
            plan.put(out, (1,), rest_in[n], lambda p: (ALL, ALL, inside))
        else:
            plan.put(out, (1,), rest_in[-1], lambda p: (ALL, n - single, ALL, inside))

    last_spans = [late]
    if late[1] >= 2 * GROUP:
        tail = GROUP * (late[1] // (2 * GROUP))
        last_spans = [(half, late[1] - tail), (rows - tail, tail)]
    late_parts = [(k, late) for k in far_masks[:-1]] + [(far_masks[-1], part) for part in last_spans]
    far = {k: [] for k in others + far_masks}

    def across(k, begin, value):
        sides = sideways(value.reshape(INNER * each, -1, depth))
        far[k].append((begin, sides))
        return sides[1]

    def crossing(pieces):
        plan.wait([v for _, _, v in pieces])
        return [across(k, begin, plan.after(v)) for k, begin, v in pieces]

    plan.wait(side_early, rest_in[: far_count - 1 + len(others)], home[1])
    sides = [sideways(plan.after(v)) for v in side_early]
    for k in far_masks[1:]:
        rest_piece(k, early)
    for k in others:
        rest_piece(k, late)
    made = plan.run()
    going = [(k, 0, outward(v, k)) for k, v in zip(far_masks[1:], made)]
    side_late = [(k, late[0], outward(v, k)) for k, v in zip(others, made[far_count - 1 :])]
    plan.wait(first)
    core_step([first])
    come = swap(plan.run()[0], "wide", 1)
    high_step([first], come)
    inward = swap(plan.run()[0], "wide", 2)
    plan.wait(denominator)
    own = plan.new(2, 2, each, half, depth)
    plan.put(own, (0, 0), first, lambda p: (ALL, p[1], p[0]))
    plan.put(own, (0, 1), come, lambda p: (0, ALL, p[1]))
    plan.put(own, (1,), inward, lambda p: (ALL, 0))
    lead_own = plan.run()[0]
    plan.wait(home[1])
    crossed = [v[1] for v in sides]
    lead_crossed = across(lead, 0, lead_own)

    for k, part in late_parts:
        rest_piece(k, late, part)
    plan.wait([v for _, _, v in going])
    late_out = plan.run()
    later = [
        (k, late[0], outward(v, k)) for (k, _), v in zip(late_parts[: far_count - 1], late_out)
    ]
    plan.wait(crossed)
    side_crossed = crossing(side_late)
    plan.wait(lead_crossed)
    crossed = crossing(going)
    for v in [home] + sides:
        core_step(v)
    comes = [swap(v, "wide", 1) for v in plan.run()]
    high_step(home, comes[0], *early)
    for v, come in zip(sides, comes[1:]):
        high_step(v, come)
    high_step(home, comes[0], *late)
    made = plan.run()
    inner = [swap(v, "wide", 2) for v in made[:-1]]

    plan.wait(crossed, inner[0])
    home_late = swap(plan.after(made[-1]), "wide", 2)
    final = [(far_masks[-1], part) for part in last_spans]
    final_out = late_out[far_count - 1 :]
    plan.wait([v for _, _, v in later])
    ending = [
        (k, part[0], outward(plan.after(v), k)) for (k, part), v in zip(final[:1], final_out)
    ]
    crossed = crossing(later)

    flat_integrals = integrals.reshape(rows_here * window, rows, depth_all)
    partials = []
    near = [[((0, 0, 0), v + [c, i]) for v, c, i in zip([home] + sides, comes, inner)]]
    near.append([((0, 0, late[0]), home + [comes[0], home_late])])

    def multiply(h, span, last):
        pieces = [
            next(v for v in reversed(far[k]) if v[0] <= span[0])
            for k in (others if h else []) + far_masks
        ]
        value = contract(
            places,
            plan.after(flat_integrals),
            near[h],
            pieces,
            partials if last else [],
            near_masks + far_masks,
            *span,
            last,
        )
        plan.before = [value]
        partials.append(value)

    part = GROUP * max(1, half // (2 * GROUP))
    multiply(0, (0, part), False)
    for (k, span), v in zip(final[1:], final_out[1:]):
        ending.append((k, span[0], outward(plan.after(v), k)))
    if part < half:
        multiply(0, (part, half - part), False)
    plan.wait(side_crossed)
    for n in range(len(ending)):
        crossing(ending[n : n + 1])
    for n, span in enumerate(last_spans):
        multiply(1, span, n == len(last_spans) - 1)
    value = partials[-1]

    sent = value.reshape((wide * narrow,) + value.shape[2:])
    got = lax.all_to_all(sent, ("wide", "narrow"), 0, 0, tiled=True)
    got = got.reshape(wide, narrow, pairs_here, rows_here, window)
    whole = jnp.sum(got, axis=0).transpose(0, 2, 3, 1).reshape(window, window, pairs_here)
    combined = whole + jnp.transpose(whole, (1, 0, 2))
    combined = lax.dynamic_slice_in_dim(combined, row_start, rows_here, 0)
    return combined / denominator


def solution(mesh):
    in_specs = (
        P("wide", None, "narrow"),
        P("narrow", None, "wide", None),
        P("wide", None),
        P(),
        P(),
        P(),
    )
    out_specs = P("narrow", None, "wide")
    return jax.shard_map(shards, mesh=mesh, in_specs=in_specs, out_specs=out_specs, check_vma=False)
```
